32 devices in a mesh: field: 2 (over x), tm: 4 (over y, core), tile: 4 (over z).
Axes of the slice: x: 2, y: 2, z: 4, core: 2. Of those that a mesh axis runs over, the one named last changes fastest.
Arguments:
- movie: bfloat16 [32, 1024, 1024], P(('field', 'tm'), 'tile'), parts along dimension 0, may hold values from -6 to 6
- patch_in: bfloat16 [16, 64], replicated, may hold values from -1.5 to 1.5
- patch_bias: float32 [64], replicated, may hold values from -3 to 3
- conv_weight: bfloat16 [2, 9, 64, 64], replicated, may hold values from -0.25 to 0.25
- conv_bias: float32 [2, 64], replicated, may hold values from -3 to 3
- patch_out: bfloat16 [64, 16], replicated, may hold values from -0.75 to 0.75
- footprint: bfloat16 [128, 64, 1024], P(('field', 'tile'), 'tm'), parts along dimension 0, may hold values from 0 to 0.0625
- slot_cell: int32 [128, 64], P(('field', 'tile')), parts along dimension 0, may hold values from 0 to 3071, as said below
- slot_window_index: int32 [128, 64], P(('field', 'tile')), parts along dimension 0, may hold values from 0 to 15
- decay: float32 [6144], P(('field', 'tm', 'tile')), parts along dimension 0, may hold values from 0.3 to 0.95
Outputs:
- activity: float32 [16, 6144], P(None, ('field', 'tm', 'tile')), parts along dimension 1
The draws below stay inside these ranges and needn't reach their ends.
There are 2 independent parts, one for each index of `field`. The reference program is written for one: setup_inputs(seed, part) draws one part's arguments, and reference() takes and returns one part's arrays. A program takes and returns all parts, laid end to end along the dimension named above; an argument that names none is the same for every part. Nothing has to cross between parts.
Inputs may be any that keep to these rules, and one draw needn't show every extreme that they name: `slot_cell`: every one of the 3072 cells is named by at least one slot.
All inputs are finite; a program needn't handle non-finite values.
Results may differ from the reference program's by a relative error of at most 0.0069.
Values may be sent and summed in bfloat16 or wider, within the bound.
No kernel may reach another device: no remote copies, remote signals or barrier semaphores. Data moves between devices by JAX's collectives and lax.ppermute only.
A program may use at most 192 MiB of HBM per device.

```python
import jax
import jax.numpy as jnp
from jax import lax

IMG = 1024
BLK = 128
WINDOW_SIDE = 32
CHAN = 64
LAYERS = 2
SLOTS_PER_BLOCK = 64
FRAMES = 16
FRAME_BLOCKS = 64
CELLS = 3072


def draw_slot_cell(key, part):
    total_count = FRAME_BLOCKS * SLOTS_PER_BLOCK
    first_key = jax.random.fold_in(key, 11)
    second_key = jax.random.fold_in(key, 23)
    extra = jax.random.randint(first_key, (total_count - CELLS,), 0, CELLS, dtype=jnp.int32)
    listed_items = jnp.concatenate([jnp.arange(CELLS, dtype=jnp.int32), extra])
    sort_order = jax.random.permutation(second_key, total_count)
    return listed_items[sort_order].reshape(FRAME_BLOCKS, SLOTS_PER_BLOCK).astype(jnp.int32)


def touch_ends(values, stream_key, least, high):
    extent = values.shape
    place = [jax.random.randint(jax.random.fold_in(stream_key, axis), (), 0, extent[axis]) for axis in range(len(extent))]
    values = values.at[tuple(place)].set(least)
    longest = extent.index(max(extent))
    place[longest] = (place[longest] + 1) % extent[longest]
    return values.at[tuple(place)].set(high)


def levels(key, dims, cuts, smallest, largest):
    gain, own = 1.0, jax.random.fold_in(key, 6)
    for dim, shards_of in cuts:
        steps = jnp.exp(jax.random.uniform(jax.random.fold_in(own, dim), (shards_of,), jnp.float32, smallest / len(cuts), largest / len(cuts)))
        gain = gain * jnp.repeat(steps, dims[dim] // shards_of).reshape([-1 if axis == dim else 1 for axis in range(len(dims))])
    return gain


def noise(rng, dims, deviation, most, pieces=(), kind=jnp.bfloat16):
    array = jax.random.normal(rng, dims, jnp.float32) * deviation
    if len(pieces) > 0:
        array = levels(rng, dims, pieces, -0.22, 0.18) * array
    return jnp.clip(array, min=-most, max=most).astype(kind)


def setup_inputs(seed: int = 0, part: int = 0) -> dict:
    streams_of = jax.random.split(jax.random.key(seed), 11)
    part_splits = jax.random.split(jax.random.fold_in(streams_of[10], part), 11)
    movie = noise(part_splits[0], (FRAMES, IMG, IMG), 1.0, 6.0, ((0, 4), (1, 4)))
    patch_in = noise(streams_of[1], (16, CHAN), 16 ** -0.5, 1.5)
    patch_bias = noise(streams_of[2], (CHAN,), 0.5, 3.0, (), jnp.float32)
    conv_weight = noise(streams_of[3], (LAYERS, 9, CHAN, CHAN), (9 * CHAN) ** -0.5, 0.25)
    conv_bias = noise(streams_of[4], (LAYERS, CHAN), 0.5, 3.0, (), jnp.float32)
    patch_out = noise(streams_of[5], (CHAN, 16), CHAN ** -0.5, 0.75)
    footprint = jnp.clip(0.0625 * jax.random.uniform(part_splits[6], (FRAME_BLOCKS, SLOTS_PER_BLOCK, WINDOW_SIDE * WINDOW_SIDE), jnp.float32) ** levels(part_splits[6], (FRAME_BLOCKS, SLOTS_PER_BLOCK, WINDOW_SIDE * WINDOW_SIDE), ((0, 4), (1, 4)), -0.2, 0.2), 0.0, 0.0625).astype(jnp.bfloat16)
    slot_cell = draw_slot_cell(jax.random.fold_in(jax.random.fold_in(streams_of[10], part), 71), part)
    slot_window_index = touch_ends(jax.random.randint(part_splits[8], (FRAME_BLOCKS, SLOTS_PER_BLOCK), 0, 16), jax.random.fold_in(part_splits[8], 1), 0, 15).astype(jnp.int32)
    decay = jnp.clip(0.3 + 0.65 * jax.random.uniform(part_splits[9], (CELLS,), jnp.float32) ** levels(part_splits[9], (CELLS,), ((0, 16),), -0.2, 0.2), 0.3, 0.95)
    return dict(movie=movie, patch_in=patch_in, patch_bias=patch_bias, conv_weight=conv_weight, conv_bias=conv_bias, patch_out=patch_out, footprint=footprint, slot_cell=slot_cell, slot_window_index=slot_window_index, decay=decay)


def conv_layer(field, weights, bias):
    coarse = field.shape[1]
    padded = jnp.pad(field, ((0, 0), (1, 1), (1, 1)))
    summed = jnp.zeros(field.shape, jnp.float32)
    for row_tap in range(3):
        for col_tap in range(3):
            window = padded[:, row_tap:row_tap + coarse, col_tap:col_tap + coarse].astype(jnp.float32)
            summed = summed + jnp.einsum('oc,crw->orw', weights[3 * row_tap + col_tap].astype(jnp.float32), window)
    return (field.astype(jnp.float32) + jax.nn.relu(summed + bias[:, None, None])).astype(jnp.bfloat16)

def denoise_frame(frame, patch_in, patch_bias, conv_weight, conv_bias, patch_out):
    coarse = IMG // 4
    pixels = frame.reshape(coarse, 4, coarse, 4).astype(jnp.float32)
    features = jnp.einsum('raub,abc->cru', pixels, patch_in.reshape(4, 4, -1).astype(jnp.float32))
    features = jax.nn.relu(features + patch_bias[:, None, None]).astype(jnp.bfloat16)
    for layer in range(LAYERS):
        features = conv_layer(features, conv_weight[layer], conv_bias[layer])
    decoded = jnp.einsum('cru,cab->raub', features.astype(jnp.float32), patch_out.reshape(-1, 4, 4).astype(jnp.float32))
    return (decoded + pixels).astype(jnp.bfloat16).reshape(IMG, IMG)

def frame_traces(denoised, footprint, slot_cell, slot_window_index):
    per_side = IMG // BLK
    win = BLK // 4
    windows = denoised.reshape(per_side, 4, win, per_side, 4, win).transpose(0, 3, 1, 4, 2, 5)
    windows = windows.reshape(per_side * per_side, 16, win * win)
    every = jnp.einsum('bsp,bqp->bsq', footprint.astype(jnp.float32), windows.astype(jnp.float32))
    slot_sums = jnp.take_along_axis(every, slot_window_index.astype(jnp.int32)[:, :, None], axis=2)[:, :, 0]
    return jax.ops.segment_sum(slot_sums.reshape(-1), slot_cell.reshape(-1), num_segments=CELLS)

def reference(movie, patch_in, patch_bias, conv_weight, conv_bias, patch_out, footprint, slot_cell, slot_window_index, decay):

    def one_frame(frame):
        denoised = denoise_frame(frame, patch_in, patch_bias, conv_weight, conv_bias, patch_out)
        return frame_traces(denoised, footprint, slot_cell, slot_window_index)
    traces = lax.map(one_frame, movie)
    centered = traces - lax.optimization_barrier(jnp.mean(traces, axis=0))[None, :]
    previous = jnp.concatenate([jnp.zeros((1, CELLS), jnp.float32), centered[:-1]], axis=0)
    spikes = centered - decay[None, :] * previous
    scale = jnp.sqrt(lax.optimization_barrier(jnp.mean(spikes * spikes, axis=0)) + 1e-05)
    return spikes / scale[None, :]
```

```python
import functools

import jax
import jax.numpy as jnp
from jax import lax
from jax.experimental import pallas as pl
from jax.experimental.pallas import tpu as pltpu
from jax.sharding import PartitionSpec as P

BLK = 128
LANES = 128
STRIP = 8
NT = (((1,), (1,)), ((), ()))
F32 = jnp.float32
BF16 = jnp.bfloat16


def conv_taps(layer):
    blocks = []
    for d in range(2):
        for side in range(2):
            for x in range(2):
                for h_in in range(2):
                    in_row = 2 * (d - 1) + h_in if layer % 2 == 0 else 2 * d - h_in
                    in_col = x if side == 0 else (-1, 2)[x]
                    row = []
                    for c in range(2):
                        for h_out in range(2):
                            out_row = -h_out if layer % 2 == 0 else h_out
                            tap_r, tap_c = in_row - out_row + 1, in_col - c + 1
                            ok = 0 <= tap_r <= 2 and 0 <= tap_c <= 2
                            row.append(3 * tap_r + tap_c if ok else None)
                    blocks.append(row)
    return blocks


def prep_kernel(patch_in_ref, conv_ref, patch_out_ref, win_ref, w1_ref, w2_ref, wd_ref):
    chan = patch_in_ref.shape[1]
    pixel = lax.broadcasted_iota(jnp.int32, (256, 16), 0)
    tap = lax.broadcasted_iota(jnp.int32, (256, 16), 1)
    sel = (((pixel // 32) % 4) * 4 + pixel % 4 == tap).astype(BF16)
    spread_in = jnp.dot(sel, patch_in_ref[...], preferred_element_type=F32)
    spread_out = lax.dot_general(patch_out_ref[...], sel, NT, preferred_element_type=F32)
    k = lax.broadcasted_iota(jnp.int32, (256, 2 * chan), 0)
    lane = lax.broadcasted_iota(jnp.int32, (256, 2 * chan), 1)
    wide_in = jnp.concatenate([spread_in, spread_in], axis=1)
    for pair in range(8):
        keep = ((k % 32) // 4 == pair) & (k // 128 == lane // chan)
        win_ref[:, pair * 2 * chan : (pair + 1) * 2 * chan] = jnp.where(keep, wide_in, 0.0).astype(BF16)
    k = lax.broadcasted_iota(jnp.int32, (2 * chan, 256), 1)
    half = lax.broadcasted_iota(jnp.int32, (2 * chan, 256), 0) // chan
    wide_out = jnp.concatenate([spread_out, spread_out], axis=0)
    for pair in range(8):
        keep = ((k % 32) // 4 == pair) & (k // 128 == half)
        wd_ref[pair * 2 * chan : (pair + 1) * 2 * chan, :] = jnp.where(keep, wide_out, 0.0).astype(BF16)
    eye = (
        lax.broadcasted_iota(jnp.int32, (chan, chan), 0)
        == lax.broadcasted_iota(jnp.int32, (chan, chan), 1)
    ).astype(BF16)
    blank = jnp.zeros((chan, chan), F32)
    for layer, out in enumerate((w1_ref, w2_ref)):
        turned = [
            lax.dot_general(eye, conv_ref[layer, tap], NT, preferred_element_type=F32)
            for tap in range(9)
        ]
        for row, taps in enumerate(conv_taps(layer)):
            for c in range(2):
                pair = [blank if taps[2 * c + h] is None else turned[taps[2 * c + h]] for h in range(2)]
                out[row * chan : (row + 1) * chan, c * LANES : (c + 1) * LANES] = jnp.concatenate(
                    pair, axis=1
                ).astype(BF16)


def prepare(patch_in, conv_weight, patch_out):
    chan = patch_in.shape[1]
    return pl.pallas_call(
        prep_kernel,
        out_shape=(
            jax.ShapeDtypeStruct((256, 16 * chan), BF16),
            jax.ShapeDtypeStruct((16 * chan, 4 * chan), BF16),
            jax.ShapeDtypeStruct((16 * chan, 4 * chan), BF16),
            jax.ShapeDtypeStruct((16 * chan, 256), BF16),
        ),
        name="prep",
    )(patch_in, conv_weight, patch_out)


def store_features(lo_ref, hi_ref, base, first, lo, hi, frames, rows):
    count = lo.shape[0] // rows
    lo_ref[base, first * rows : (first + count) * rows, :] = lo.astype(BF16)
    hi_ref[base, (first + 1) * rows : (first + count + 1) * rows, :] = hi.astype(BF16)
    group = lax.broadcasted_iota(jnp.int32, (rows, LANES), 0) % (rows // frames)
    if first == 0:
        up = pltpu.roll(lo[0:rows], rows - 1, 0)
        up = jnp.where(group == rows // frames - 1, 0.0, up)
        lo_ref[base, 16 * rows : 17 * rows, :] = up.astype(BF16)
    if first + count == 16:
        down = pltpu.roll(hi[(count - 1) * rows : count * rows], 1, 0)
        down = jnp.where(group == 0, 0.0, down)
        hi_ref[base, 0:rows, :] = down.astype(BF16)


def gather_rows(lo_ref, hi_ref, base, start, size, rows):
    a, b = start, start + size
    return [
        lo_ref[base, a:b, :],
        hi_ref[base, a + rows : b + rows, :],
        hi_ref[base, a:b, :],
        lo_ref[base, a + rows : b + rows, :],
    ]


def denoise_kernel(
    strips,
    frames,
    masked,
    flags_ref,
    movie_ref,
    win_ref,
    w1_ref,
    w2_ref,
    wd_ref,
    patch_bias_ref,
    conv_bias_ref,
    out_ref,
    z_ref,
    x_ref,
    f0lo_ref,
    f0hi_ref,
    f1lo_ref,
    f1hi_ref,
):
    blocks = movie_ref.shape[2] // LANES
    rows = frames * blocks
    m = 16 * rows
    lane = lax.broadcasted_iota(jnp.int32, (rows, LANES), 1)
    odd_chunk = (lane // 32) % 2 == 1
    high_chunk = lane // 64 == 1
    step = pl.program_id(0)

    for ref in (f0lo_ref, f0hi_ref, f1lo_ref, f1hi_ref, x_ref):
        ref[0] = ref[strips]

    scale = [None] * strips
    odd_scale = [None] * strips
    even_scale = [None] * strips
    if masked:
        first = step == 0
        last = step == pl.num_programs(0) - 1
        top = jnp.where(first, flags_ref[0], 1.0)
        bottom = jnp.where(last, flags_ref[1], 1.0)
        scale[0] = top
        scale[strips - 1] = bottom
        odd_scale[strips - 1] = top
        even_scale[strips - 1] = bottom

    for s in range(strips):
        for f in range(frames):
            pixels = movie_ref[f, s * STRIP : (s + 1) * STRIP, :].astype(F32)
            for t in range(blocks):
                z_ref[s, (f * blocks + t) * STRIP : (f * blocks + t + 1) * STRIP, :] = pixels[
                    :, t * LANES : (t + 1) * LANES
                ]
    for s in range(strips):
        halves = []
        for g in range(2):
            a = [z_ref[s, pl.ds(4 * g + p, rows, stride=STRIP), :] for p in range(4)]
            b = [None] * 4
            for p in (0, 2):
                b[p] = jnp.where(odd_chunk, pltpu.roll(a[p + 1], 32, 1), a[p])
                b[p + 1] = jnp.where(odd_chunk, a[p + 1], pltpu.roll(a[p], LANES - 32, 1))
            c = [None] * 4
            for p in (0, 1):
                c[p] = jnp.where(high_chunk, pltpu.roll(b[p + 2], 64, 1), b[p])
                c[p + 2] = jnp.where(high_chunk, b[p + 2], pltpu.roll(b[p], LANES - 64, 1))
            halves.append(c)
        for q in range(4):
            x_ref[s + 1, q * rows : (q + 1) * rows, 0:LANES] = halves[0][q].astype(BF16)
            x_ref[s + 1, q * rows : (q + 1) * rows, LANES : 2 * LANES] = halves[1][q].astype(BF16)

    for s in range(strips):
        summed = jnp.dot(x_ref[s + 1], win_ref[...], preferred_element_type=F32)
        bias = patch_bias_ref[...]
        for q in range(4):
            for j in range(4):
                part = summed[q * rows : (q + 1) * rows, j * 256 : (j + 1) * 256]
                part = jnp.maximum(part + bias, 0.0)
                if scale[s] is not None:
                    part = part * scale[s]
                store_features(
                    f0lo_ref, f0hi_ref, s + 1, 4 * q + j, part[:, 0:LANES], part[:, LANES:], frames, rows
                )

    lane_m = lax.broadcasted_iota(jnp.int32, (m, LANES), 1) < 64

    for s in range(strips):
        pieces = gather_rows(f0lo_ref, f0hi_ref, s, 0, m, rows) + gather_rows(
            f0lo_ref, f0hi_ref, s + 1, 0, m, rows
        )
        summed = jnp.dot(
            jnp.concatenate(pieces, axis=1), w1_ref[...], preferred_element_type=F32
        )
        summed = jnp.maximum(summed + conv_bias_ref[0:1, :], 0.0)
        new = []
        for c in range(2):
            kept = jnp.where(lane_m, pieces[4 + c].astype(F32), pieces[c].astype(F32))
            value = kept + summed[:, c * LANES : (c + 1) * LANES]
            if even_scale[s] is not None:
                value = value * jnp.where(lane_m, even_scale[s], odd_scale[s])
            new.append(value)
        store_features(f1lo_ref, f1hi_ref, s + 1, 0, new[0], new[1], frames, rows)

    for s in range(strips):
        pieces = gather_rows(f1lo_ref, f1hi_ref, s, 0, m, rows) + gather_rows(
            f1lo_ref, f1hi_ref, s + 1, 0, m, rows
        )
        summed = jnp.dot(
            jnp.concatenate(pieces, axis=1), w2_ref[...], preferred_element_type=F32
        )
        summed = jnp.maximum(summed + conv_bias_ref[1:2, :], 0.0)
        new = []
        for c in range(2):
            kept = jnp.where(lane_m, pieces[c].astype(F32), pieces[4 + c].astype(F32))
            new.append((kept + summed[:, c * LANES : (c + 1) * LANES]).astype(BF16))
        wide = []
        for q in range(4):
            parts = []
            for j in range(4):
                at = (4 * q + j) * rows
                parts += [new[0][at : at + rows], new[1][at : at + rows]]
            wide.append(jnp.concatenate(parts, axis=1))
        decoded = jnp.dot(
            jnp.concatenate(wide, axis=0), wd_ref[...], preferred_element_type=F32
        )
        out_ref[s] = (decoded + x_ref[s].astype(F32)).astype(BF16)


def denoise(movie, flags, weights, patch_bias, conv_bias, strips, masked, name):
    frames, height, width = movie.shape
    total = height // STRIP
    rows = frames * (width // LANES)
    grid = total // strips
    win, w1, w2, wd = weights
    whole = lambda a: pl.BlockSpec(a.shape, lambda n: (0,) * a.ndim)
    flops = 2 * total * rows * 16 * (2 * 1024 * 256 + 256 * 256 + 256 * 256)
    return pl.pallas_call(
        functools.partial(denoise_kernel, strips, frames, masked),
        grid=(grid,),
        in_specs=[
            pl.BlockSpec(memory_space=pltpu.SMEM),
            pl.BlockSpec((frames, strips * STRIP, width), lambda n: (0, n, 0)),
            whole(win),
            whole(w1),
            whole(w2),
            whole(wd),
            whole(patch_bias),
            whole(conv_bias),
        ],
        out_specs=pl.BlockSpec((strips, 4 * rows, 256), lambda n: (n, 0, 0)),
        out_shape=jax.ShapeDtypeStruct((total, 4 * rows, 256), BF16),
        scratch_shapes=[
            pltpu.VMEM((strips, rows * STRIP, LANES), F32),
            pltpu.VMEM((strips + 1, 4 * rows, 256), BF16),
        ]
        + [pltpu.VMEM((strips + 1, 17 * rows, LANES), BF16)] * 4,
        compiler_params=pltpu.CompilerParams(vmem_limit_bytes=48 << 20),
        cost_estimate=pl.CostEstimate(flops=flops, bytes_accessed=8 << 20, transcendentals=0),
        name=name,
    )(flags, movie, win, w1, w2, wd, patch_bias, conv_bias)


def cells_kernel(frames, own, inner_ref, edge_ref, footprint_ref, cell_ref, window_ref, out_ref):
    total = inner_ref.shape[0]
    rows4 = inner_ref.shape[1]
    rows = rows4 // 4
    blocks = rows // frames
    slots = footprint_ref.shape[1]
    n = blocks * slots
    owned = out_ref.shape[0]
    group = lax.broadcasted_iota(jnp.int32, (blocks, n), 0)
    acc = None
    for kb in range(total // 16):
        lhs = []
        for iw in range(4):
            parts = []
            for i4 in range(4):
                i = 16 * kb + 4 * iw + i4
                if i == 0:
                    parts.append(edge_ref[2])
                elif i == total - 1:
                    parts.append(edge_ref[5])
                else:
                    parts.append(inner_ref[i + 1])
            lhs.append(jnp.concatenate(parts, axis=1))
        weights = footprint_ref[kb * blocks : (kb + 1) * blocks].reshape(n, footprint_ref.shape[2])
        every = lax.dot_general(
            jnp.concatenate(lhs, axis=0), weights, NT, preferred_element_type=F32
        )
        block_of = lax.broadcasted_iota(jnp.int32, (1, n), 1) // slots
        target = window_ref[kb : kb + 1, :] * blocks + block_of
        sums = []
        for f in range(frames):
            total_f = jnp.zeros((blocks, n), F32)
            for w in range(16):
                at = w * rows + f * blocks
                total_f = total_f + jnp.where(
                    target == group + w * blocks, every[at : at + blocks, :], 0.0
                )
            sums.append(jnp.sum(total_f, axis=0, keepdims=True))
        slot_sums = jnp.concatenate(sums, axis=0)
        cell = cell_ref[kb : kb + 1, :]
        owner = jnp.floor((cell.astype(F32) + 0.5) * (1.0 / own)).astype(jnp.int32)
        low = cell - owner * own
        row_owner = lax.broadcasted_iota(jnp.int32, (owned, n), 0) // frames
        onehot = jnp.where(
            lax.broadcasted_iota(jnp.int32, (own, n), 0) == low, 1.0, 0.0
        ).astype(BF16)
        spread = jnp.where(
            row_owner == owner, jnp.concatenate([slot_sums] * (owned // frames), axis=0), 0.0
        )
        for _ in range(3):
            piece = spread.astype(BF16)
            spread = spread - piece.astype(F32)
            part = lax.dot_general(piece, onehot, NT, preferred_element_type=F32)
            acc = part if acc is None else acc + part
    out_ref[...] = acc


def cells(inner, edge, footprint, slot_cell, window, frames, own, owners):
    blocks = inner.shape[1] // (4 * frames)
    return pl.pallas_call(
        functools.partial(cells_kernel, frames, own),
        out_shape=jax.ShapeDtypeStruct((owners * frames, own), F32),
        compiler_params=pltpu.CompilerParams(vmem_limit_bytes=48 << 20),
        cost_estimate=pl.CostEstimate(flops=2 << 30, bytes_accessed=5 << 20, transcendentals=0),
        name="cells",
    )(inner, edge, footprint, slot_cell.reshape(-1, blocks * slot_cell.shape[1]),
      window.reshape(-1, blocks * window.shape[1]))


def spikes_kernel(tm, tile, frames, moved_ref, decay_ref, out_ref):
    own = out_ref.shape[1]
    pieces = []
    for a in range(tm):
        total = jnp.zeros((frames, own), F32)
        for b in range(tile):
            at = (a * tile + b) * frames
            total = total + moved_ref[at : at + frames, :]
        pieces.append(total)
    traces = jnp.concatenate(pieces, axis=0)
    count = tm * frames
    centered = traces - jnp.sum(traces, axis=0, keepdims=True) * (1.0 / count)
    previous = jnp.concatenate([jnp.zeros((1, own), F32), centered[:-1]], axis=0)
    spikes = centered - decay_ref[...] * previous
    power = jnp.sum(spikes * spikes, axis=0, keepdims=True) * (1.0 / count)
    out_ref[...] = spikes / jnp.sqrt(power + 1e-05)


def body(
    movie,
    patch_in,
    patch_bias,
    conv_weight,
    conv_bias,
    patch_out,
    footprint,
    slot_cell,
    slot_window_index,
    decay,
):
    frames = movie.shape[0]
    own = decay.shape[0]
    tm, tile = lax.axis_size("tm"), lax.axis_size("tile")
    place = lax.axis_index("tile")
    forward = [(i, i + 1) for i in range(tile - 1)]
    backward = [(target, source) for source, target in forward]
    above = lax.ppermute(movie[:, -STRIP:], "tile", forward)
    below = lax.ppermute(movie[:, :STRIP], "tile", backward)
    slots = lax.all_gather(footprint, "tm", axis=1, tiled=True)
    weights = prepare(patch_in, conv_weight, patch_out)
    bias0 = jnp.tile(patch_bias[None, :], (1, 4))
    bias12 = jnp.tile(conv_bias, (1, 4))
    flags = jnp.stack([place > 0, place < tile - 1]).astype(F32)
    inner = denoise(movie, flags, weights, bias0, bias12, 2, False, "inner")
    rim = jnp.concatenate(
        [above, movie[:, : 2 * STRIP], movie[:, -2 * STRIP :], below], axis=1
    )
    edge = denoise(rim, flags, weights, bias0, bias12, 2, True, "edge")
    per_cell = cells(inner, edge, slots, slot_cell, slot_window_index, frames, own, tm * tile)
    moved = lax.all_to_all(per_cell, ("tm", "tile"), split_axis=0, concat_axis=0, tiled=True)
    return pl.pallas_call(
        functools.partial(spikes_kernel, tm, tile, frames),
        out_shape=jax.ShapeDtypeStruct((tm * frames, own), F32),
        name="spikes",
    )(moved, decay[None, :])


def solution(mesh):
    placed = (
        P(("field", "tm"), "tile", None),
        P(),
        P(),
        P(),
        P(),
        P(),
        P(("field", "tile"), "tm", None),
        P(("field", "tile"), None),
        P(("field", "tile"), None),
        P(("field", "tm", "tile")),
    )
    return jax.shard_map(
        body,
        mesh=mesh,
        in_specs=placed,
        out_specs=P(None, ("field", "tm", "tile")),
        check_vma=False,
    )
```

```python
import functools

import jax
import jax.numpy as jnp
from jax import lax
from jax.experimental import pallas as pl
from jax.experimental.pallas import tpu as pltpu
from jax.sharding import PartitionSpec as P

BLK = 128
LANES = 128
STRIP = 8
STRIPS = 4
VMEM_BYTES = 60 << 20
NT = (((1,), (1,)), ((), ()))
F32 = jnp.float32
BF16 = jnp.bfloat16


def conv_taps(layer):
    blocks = []
    for d in range(2):
        for side in range(2):
            for x in range(2):
                for h_in in range(2):
                    in_row = 2 * (d - 1) + h_in if layer % 2 == 0 else 2 * d - h_in
                    in_col = x if side == 0 else (-1, 2)[x]
                    row = []
                    for c in range(2):
                        for h_out in range(2):
                            out_row = -h_out if layer % 2 == 0 else h_out
                            tap_r, tap_c = in_row - out_row + 1, in_col - c + 1
                            ok = 0 <= tap_r <= 2 and 0 <= tap_c <= 2
                            row.append(3 * tap_r + tap_c if ok else None)
                    blocks.append(row)
    return blocks


def prepare(patch_in_ref, conv_ref, patch_out_ref, win_ref, w1_ref, w2_ref, wd_ref):
    chan = patch_in_ref.shape[1]
    pixel = lax.broadcasted_iota(jnp.int32, (256, 16), 0)
    tap = lax.broadcasted_iota(jnp.int32, (256, 16), 1)
    sel = (((pixel // 32) % 4) * 4 + pixel % 4 == tap).astype(BF16)
    spread_in = jnp.dot(sel, patch_in_ref[...], preferred_element_type=F32)
    spread_out = lax.dot_general(patch_out_ref[...], sel, NT, preferred_element_type=F32)
    k = lax.broadcasted_iota(jnp.int32, (256, 2 * chan), 0)
    lane = lax.broadcasted_iota(jnp.int32, (256, 2 * chan), 1)
    wide_in = jnp.concatenate([spread_in, spread_in], axis=1)
    for pair in range(8):
        keep = ((k % 32) // 4 == pair) & (k // 128 == lane // chan)
        win_ref[:, pair * 2 * chan : (pair + 1) * 2 * chan] = jnp.where(keep, wide_in, 0.0).astype(BF16)
    k = lax.broadcasted_iota(jnp.int32, (2 * chan, 256), 1)
    half = lax.broadcasted_iota(jnp.int32, (2 * chan, 256), 0) // chan
    wide_out = jnp.concatenate([spread_out, spread_out], axis=0)
    for pair in range(8):
        keep = ((k % 32) // 4 == pair) & (k // 128 == half)
        wd_ref[pair * 2 * chan : (pair + 1) * 2 * chan, :] = jnp.where(keep, wide_out, 0.0).astype(BF16)
    eye = (
        lax.broadcasted_iota(jnp.int32, (chan, chan), 0)
        == lax.broadcasted_iota(jnp.int32, (chan, chan), 1)
    ).astype(BF16)
    blank = jnp.zeros((chan, chan), F32)
    for layer, out in enumerate((w1_ref, w2_ref)):
        turned = [
            lax.dot_general(eye, conv_ref[layer, tap], NT, preferred_element_type=F32)
            for tap in range(9)
        ]
        for row, taps in enumerate(conv_taps(layer)):
            for c in range(2):
                pair = [blank if taps[2 * c + h] is None else turned[taps[2 * c + h]] for h in range(2)]
                out[row * chan : (row + 1) * chan, c * LANES : (c + 1) * LANES] = jnp.concatenate(
                    pair, axis=1
                ).astype(BF16)


def denoise_kernel(
    strips,
    movie_ref,
    above_ref,
    below_ref,
    patch_in_ref,
    patch_bias_ref,
    conv_ref,
    conv_bias_ref,
    patch_out_ref,
    out_ref,
    win_ref,
    w1_ref,
    w2_ref,
    wd_ref,
    z_ref,
    x_ref,
    f0lo_ref,
    f0hi_ref,
    f1lo_ref,
    f1hi_ref,
    f2_ref,
):
    frames = movie_ref.shape[0]
    blocks = movie_ref.shape[2] // LANES
    rows = frames * blocks
    m = 16 * rows
    lane = lax.broadcasted_iota(jnp.int32, (rows, LANES), 1)
    group = lax.broadcasted_iota(jnp.int32, (rows, LANES), 0) % blocks
    odd_chunk = (lane // 32) % 2 == 1
    high_chunk = lane // 64 == 1
    step = pl.program_id(0)
    last = pl.num_programs(0) - 1
    place = lax.axis_index("tile")
    top = jnp.where(place > 0, 1.0, 0.0)
    bottom = jnp.where(place < lax.axis_size("tile") - 1, 1.0, 0.0)

    def relayout(source_ref, row, slot, z):
        for f in range(frames):
            pixels = source_ref[f, row : row + STRIP, :].astype(F32)
            for t in range(blocks):
                at = (f * blocks + t) * STRIP
                z_ref[z, at : at + STRIP, :] = pixels[:, t * LANES : (t + 1) * LANES]
        for g in range(2):
            a = [z_ref[z, pl.ds(4 * g + p, rows, stride=STRIP), :] for p in range(4)]
            b = [None] * 4
            for p in (0, 2):
                b[p] = jnp.where(odd_chunk, pltpu.roll(a[p + 1], 32, 1), a[p])
                b[p + 1] = jnp.where(odd_chunk, a[p + 1], pltpu.roll(a[p], LANES - 32, 1))
            for p in (0, 1):
                low = jnp.where(high_chunk, pltpu.roll(b[p + 2], 64, 1), b[p])
                high = jnp.where(high_chunk, b[p + 2], pltpu.roll(b[p], LANES - 64, 1))
                for q, value in ((p, low), (p + 2, high)):
                    x_ref[slot, q * rows : (q + 1) * rows, g * LANES : (g + 1) * LANES] = value.astype(BF16)

    def store(lo_ref, hi_ref, slot, jj, lo, hi):
        lo_ref[slot, jj * rows : (jj + 1) * rows, :] = lo.astype(BF16)
        hi_ref[slot, (jj + 1) * rows : (jj + 2) * rows, :] = hi.astype(BF16)
        if jj == 0:
            up = jnp.where(group == blocks - 1, 0.0, pltpu.roll(lo, rows - 1, 0))
            lo_ref[slot, 16 * rows : 17 * rows, :] = up.astype(BF16)
        if jj == 15:
            down = jnp.where(group == 0, 0.0, pltpu.roll(hi, 1, 0))
            hi_ref[slot, 0:rows, :] = down.astype(BF16)

    def embed(start, count, scale):
        summed = jnp.dot(
            x_ref[start : start + count].reshape(count * 4 * rows, 256),
            win_ref[...],
            preferred_element_type=F32,
        )
        bias = jnp.concatenate([patch_bias_ref[...]] * 4, axis=1)
        for s in range(count):
            for q in range(4):
                for j in range(4):
                    at = (s * 4 + q) * rows
                    part = jnp.maximum(summed[at : at + rows, j * 256 : (j + 1) * 256] + bias, 0.0)
                    if scale is not None:
                        part = part * scale
                    store(f0lo_ref, f0hi_ref, start + s, 4 * q + j, part[:, 0:LANES], part[:, LANES:])

    def gather(lo_ref, hi_ref, start, count):
        def take(ref, offset):
            return ref[start : start + count, offset : offset + m, :].reshape(count * m, LANES)

        return [take(lo_ref, 0), take(hi_ref, rows), take(hi_ref, 0), take(lo_ref, rows)]

    def conv(lo_ref, hi_ref, weights_ref, layer, count):
        first = gather(lo_ref, hi_ref, 0, count)
        second = gather(lo_ref, hi_ref, 1, count)
        summed = jnp.dot(
            jnp.concatenate(first + second, axis=1), weights_ref[...], preferred_element_type=F32
        )
        bias = jnp.concatenate([conv_bias_ref[layer : layer + 1, :]] * 4, axis=1)
        even = lane < 64
        for s in range(count):
            for jj in range(16):
                at = s * m + jj * rows
                part = jnp.maximum(summed[at : at + rows] + bias, 0.0)
                halves = []
                for c in range(2):
                    below = first[c][at : at + rows].astype(F32)
                    above = second[c][at : at + rows].astype(F32)
                    kept = jnp.where(even, above, below) if layer == 0 else jnp.where(even, below, above)
                    halves.append(kept + part[:, c * LANES : (c + 1) * LANES])
                yield s, jj, halves

    def process(count, scale, row_scale):
        embed(1, count, scale)
        for s, jj, halves in conv(f0lo_ref, f0hi_ref, w1_ref, 0, count):
            if s == 0:
                halves = [half * row_scale for half in halves]
            store(f1lo_ref, f1hi_ref, s + 1, jj, *halves)
        for s, jj, halves in conv(f1lo_ref, f1hi_ref, w2_ref, 1, count):
            q, j = jj // 4, jj % 4
            for c in range(2):
                at = j * 256 + c * LANES
                f2_ref[s, q * rows : (q + 1) * rows, at : at + LANES] = halves[c].astype(BF16)
        decoded = jnp.dot(
            f2_ref[0:count].reshape(count * 4 * rows, 1024), wd_ref[...], preferred_element_type=F32
        )
        for s in range(count):
            part = decoded[s * 4 * rows : (s + 1) * 4 * rows]
            out_ref[s] = (part + x_ref[s].astype(F32)).astype(BF16)

    @pl.when(step == 0)
    def _():
        prepare(patch_in_ref, conv_ref, patch_out_ref, win_ref, w1_ref, w2_ref, wd_ref)
        relayout(above_ref, 0, 0, 0)
        embed(0, 1, top)

    @pl.when(step > 0)
    def _():
        for ref in (f0lo_ref, f0hi_ref, f1lo_ref, f1hi_ref, x_ref):
            ref[0] = ref[strips]

    @pl.when(step < last)
    def _():
        for s in range(strips):
            relayout(movie_ref, s * STRIP, s + 1, s)
        process(strips, None, jnp.where(lane < 64, 1.0, jnp.where(step == 0, top, 1.0)))

    @pl.when(step == last)
    def _():
        relayout(below_ref, 0, 1, 0)
        process(1, bottom, jnp.where(lane < 64, bottom, 1.0))


def denoise(movie, above, below, patch_in, patch_bias, conv_weight, conv_bias, patch_out, strips):
    frames, height, width = movie.shape
    total = height // STRIP
    rows = frames * (width // LANES)
    grid = total // strips
    whole = lambda a: pl.BlockSpec(a.shape, lambda n: (0,) * a.ndim)
    flops = 2 * total * rows * 16 * (2 * 1024 * 256 + 256 * 256 + 256 * 256)
    return pl.pallas_call(
        functools.partial(denoise_kernel, strips),
        grid=(grid + 1,),
        in_specs=[
            pl.BlockSpec((frames, strips * STRIP, width), lambda n: (0, jnp.minimum(n, grid - 1), 0)),
            whole(above),
            whole(below),
            whole(patch_in),
            whole(patch_bias),
            whole(conv_weight),
            whole(conv_bias),
            whole(patch_out),
        ],
        out_specs=pl.BlockSpec((strips, 4 * rows, 256), lambda n: (n, 0, 0)),
        out_shape=jax.ShapeDtypeStruct((total + strips, 4 * rows, 256), BF16),
        scratch_shapes=[
            pltpu.VMEM((256, 1024), BF16),
            pltpu.VMEM((1024, 256), BF16),
            pltpu.VMEM((1024, 256), BF16),
            pltpu.VMEM((1024, 256), BF16),
            pltpu.VMEM((strips, rows * STRIP, LANES), F32),
            pltpu.VMEM((strips + 1, 4 * rows, 256), BF16),
        ]
        + [pltpu.VMEM((strips + 1, 17 * rows, LANES), BF16)] * 4
        + [pltpu.VMEM((strips, 4 * rows, 1024), BF16)],
        compiler_params=pltpu.CompilerParams(vmem_limit_bytes=VMEM_BYTES),
        cost_estimate=pl.CostEstimate(flops=flops, bytes_accessed=8 << 20, transcendentals=0),
        name="denoise",
    )(movie, above, below, patch_in, patch_bias, conv_weight, conv_bias, patch_out)


def cells_kernel(frames, own, denoised_ref, footprint_ref, cell_ref, window_ref, out_ref):
    rows = denoised_ref.shape[1] // 4
    blocks = rows // frames
    slots = footprint_ref.shape[1]
    n = blocks * slots
    owned = out_ref.shape[0]
    kb = pl.program_id(0)

    def flat(ref):
        return jnp.concatenate([ref[pl.ds(kb * blocks + t, 1), :] for t in range(blocks)], axis=1)

    lhs = []
    for iw in range(4):
        lhs.append(
            jnp.concatenate([denoised_ref[16 * kb + 4 * iw + i4 + 1] for i4 in range(4)], axis=1)
        )
    weights = footprint_ref[...].reshape(n, footprint_ref.shape[2])
    every = lax.dot_general(jnp.concatenate(lhs, axis=0), weights, NT, preferred_element_type=F32)
    group = lax.broadcasted_iota(jnp.int32, (blocks, n), 0)
    block_of = lax.broadcasted_iota(jnp.int32, (1, n), 1) // slots
    target = flat(window_ref) * blocks + block_of
    sums = []
    for f in range(frames):
        total = jnp.zeros((blocks, n), F32)
        for w in range(16):
            at = w * rows + f * blocks
            total = total + jnp.where(target == group + w * blocks, every[at : at + blocks, :], 0.0)
        sums.append(jnp.sum(total, axis=0, keepdims=True))
    slot_sums = jnp.concatenate(sums, axis=0)
    cell = flat(cell_ref)
    owner = jnp.floor((cell.astype(F32) + 0.5) * (1.0 / own)).astype(jnp.int32)
    low = cell - owner * own
    row_owner = lax.broadcasted_iota(jnp.int32, (owned, n), 0) // frames
    onehot = jnp.where(lax.broadcasted_iota(jnp.int32, (own, n), 0) == low, 1.0, 0.0).astype(BF16)
    spread = jnp.where(
        row_owner == owner, jnp.concatenate([slot_sums] * (owned // frames), axis=0), 0.0
    )
    acc = None
    for _ in range(3):
        piece = spread.astype(BF16)
        spread = spread - piece.astype(F32)
        part = lax.dot_general(piece, onehot, NT, preferred_element_type=F32)
        acc = part if acc is None else acc + part

    @pl.when(kb == 0)
    def _():
        out_ref[...] = acc

    @pl.when(kb > 0)
    def _():
        out_ref[...] = out_ref[...] + acc


def cells(denoised, footprint, slot_cell, window, frames, own, owners):
    padded, rows4, _ = denoised.shape
    blocks = rows4 // (4 * frames)
    count, slots, pixels = footprint.shape
    whole = lambda a: pl.BlockSpec(a.shape, lambda n: (0,) * a.ndim)
    return pl.pallas_call(
        functools.partial(cells_kernel, frames, own),
        grid=(count // blocks,),
        in_specs=[
            whole(denoised),
            pl.BlockSpec((blocks, slots, pixels), lambda n: (n, 0, 0)),
            whole(slot_cell),
            whole(window),
        ],
        out_specs=pl.BlockSpec((owners * frames, own), lambda n: (0, 0)),
        out_shape=jax.ShapeDtypeStruct((owners * frames, own), F32),
        compiler_params=pltpu.CompilerParams(vmem_limit_bytes=VMEM_BYTES),
        cost_estimate=pl.CostEstimate(flops=2 << 30, bytes_accessed=5 << 20, transcendentals=0),
        name="cells",
    )(denoised, footprint, slot_cell, window)


def spikes_kernel(tm, tile, frames, moved_ref, decay_ref, out_ref):
    own = out_ref.shape[1]
    pieces = []
    for a in range(tm):
        total = jnp.zeros((frames, own), F32)
        for b in range(tile):
            at = (a * tile + b) * frames
            total = total + moved_ref[at : at + frames, :]
        pieces.append(total)
    traces = jnp.concatenate(pieces, axis=0)
    count = tm * frames
    centered = traces - jnp.sum(traces, axis=0, keepdims=True) * (1.0 / count)
    previous = jnp.concatenate([jnp.zeros((1, own), F32), centered[:-1]], axis=0)
    spikes = centered - decay_ref[...] * previous
    power = jnp.sum(spikes * spikes, axis=0, keepdims=True) * (1.0 / count)
    out_ref[...] = spikes / jnp.sqrt(power + 1e-05)


def body(
    movie,
    patch_in,
    patch_bias,
    conv_weight,
    conv_bias,
    patch_out,
    footprint,
    slot_cell,
    slot_window_index,
    decay,
):
    frames = movie.shape[0]
    own = decay.shape[0]
    tm, tile = lax.axis_size("tm"), lax.axis_size("tile")
    forward = [(i, i + 1) for i in range(tile - 1)]
    backward = [(target, source) for source, target in forward]
    above = lax.ppermute(movie[:, -STRIP:], "tile", forward)
    below = lax.ppermute(movie[:, :STRIP], "tile", backward)
    slots = lax.all_gather(footprint, "tm", axis=1, tiled=True)
    denoised = denoise(
        movie,
        above,
        below,
        patch_in,
        patch_bias[None, :],
        conv_weight,
        conv_bias,
        patch_out,
        STRIPS if movie.shape[1] % (STRIPS * STRIP) == 0 else 2,
    )
    per_cell = cells(denoised, slots, slot_cell, slot_window_index, frames, own, tm * tile)
    moved = lax.all_to_all(per_cell, ("tm", "tile"), split_axis=0, concat_axis=0, tiled=True)
    return pl.pallas_call(
        functools.partial(spikes_kernel, tm, tile, frames),
        out_shape=jax.ShapeDtypeStruct((tm * frames, own), F32),
        name="spikes",
    )(moved, decay[None, :])


def solution(mesh):
    placed = (
        P(("field", "tm"), "tile", None),
        P(),
        P(),
        P(),
        P(),
        P(),
        P(("field", "tile"), "tm", None),
        P(("field", "tile"), None),
        P(("field", "tile"), None),
        P(("field", "tm", "tile")),
    )
    return jax.shard_map(
        body,
        mesh=mesh,
        in_specs=placed,
        out_specs=P(None, ("field", "tm", "tile")),
        check_vma=False,
    )
```

```python
import functools

import jax
import jax.numpy as jnp
from jax import lax
from jax.experimental import pallas as pl
from jax.experimental.pallas import tpu as pltpu
from jax.sharding import PartitionSpec as P

BLK = 128
LANES = 128
STRIP = 8
PAD = 3
CHUNK = 64
VMEM_BYTES = 60 << 20
NT = (((1,), (1,)), ((), ()))
F32 = jnp.float32
BF16 = jnp.bfloat16


def conv_taps(layer):
    blocks = []
    for d in range(2):
        for side in range(2):
            for x in range(2):
                for h_in in range(2):
                    in_row = 2 * (d - 1) + h_in if layer % 2 == 0 else 2 * d - h_in
                    in_col = x if side == 0 else (-1, 2)[x]
                    row = []
                    for c in range(2):
                        for h_out in range(2):
                            out_row = -h_out if layer % 2 == 0 else h_out
                            tap_r, tap_c = in_row - out_row + 1, in_col - c + 1
                            ok = 0 <= tap_r <= 2 and 0 <= tap_c <= 2
                            row.append(3 * tap_r + tap_c if ok else None)
                    blocks.append(row)
    return blocks


def prepare(patch_in_ref, conv_ref, patch_out_ref, win_ref, w1_ref, w2_ref, wd_ref):
    chan = patch_in_ref.shape[1]

    def spread(taps):
        parts = [jnp.concatenate([taps[4 * a : 4 * a + 4]] * 8, axis=0) for a in range(4)]
        return jnp.concatenate(parts * 2, axis=0)

    spread_in = spread(patch_in_ref[...].astype(F32))
    spread_out = spread(patch_out_ref[...].astype(F32).T).T
    k = lax.broadcasted_iota(jnp.int32, (256, 2 * chan), 0)
    lane = lax.broadcasted_iota(jnp.int32, (256, 2 * chan), 1)
    wide_in = jnp.concatenate([spread_in, spread_in], axis=1)
    for pair in range(8):
        keep = ((k % 32) // 4 == pair) & (k // 128 == lane // chan)
        win_ref[:, pair * 2 * chan : (pair + 1) * 2 * chan] = jnp.where(keep, wide_in, 0.0).astype(BF16)
    k = lax.broadcasted_iota(jnp.int32, (2 * chan, 256), 1)
    half = lax.broadcasted_iota(jnp.int32, (2 * chan, 256), 0) // chan
    wide_out = jnp.concatenate([spread_out, spread_out], axis=0)
    for pair in range(8):
        keep = ((k % 32) // 4 == pair) & (k // 128 == half)
        wd_ref[pair * 2 * chan : (pair + 1) * 2 * chan, :] = jnp.where(keep, wide_out, 0.0).astype(BF16)
    blank = jnp.zeros((chan, chan), F32)
    for layer, out in enumerate((w1_ref, w2_ref)):
        turned = [conv_ref[layer, tap].astype(F32).T for tap in range(9)]
        for row, taps in enumerate(conv_taps(layer)):
            for c in range(2):
                pair = [blank if taps[2 * c + h] is None else turned[taps[2 * c + h]] for h in range(2)]
                out[row * chan : (row + 1) * chan, c * LANES : (c + 1) * LANES] = jnp.concatenate(
                    pair, axis=1
                ).astype(BF16)


def spread_jobs(units, jobs, lead=0, rate=None):
    done = 0
    for at, unit in enumerate(units):
        want = lead + (at * (len(jobs) - lead) // len(units) if rate is None else at * rate)
        while done < min(want, len(jobs)):
            jobs[done]()
            done += 1
        unit()
    for job in jobs[done:]:
        job()


def denoise_kernel(
    movie_ref,
    above_ref,
    below_ref,
    patch_in_ref,
    patch_bias_ref,
    conv_ref,
    conv_bias_ref,
    patch_out_ref,
    out_ref,
    win_ref,
    w1_ref,
    w2_ref,
    wd_ref,
    bias_ref,
    z_ref,
    x_ref,
    f0lo_ref,
    f0hi_ref,
    f1lo_ref,
    f1hi_ref,
    f2_ref,
):
    frames = movie_ref.shape[0]
    total = movie_ref.shape[1] // STRIP
    blocks = movie_ref.shape[2] // LANES
    rows = frames * blocks
    m = 16 * rows
    patch_rows = 2 * 4 * rows
    steps = total // 2 + 1
    lane = lax.broadcasted_iota(jnp.int32, (rows, LANES), 1)
    group = lax.broadcasted_iota(jnp.int32, (rows, LANES), 0) % blocks
    odd_chunk = (lane // 32) % 2 == 1
    high_chunk = lane // 64 == 1
    even = lane < 64
    place = lax.axis_index("tile")
    top = jnp.where(place > 0, 1.0, 0.0)
    bottom = jnp.where(place < lax.axis_size("tile") - 1, 1.0, 0.0)
    per = CHUNK // rows

    def relayout(source_ref, row, slot, z):
        for f in range(frames):
            pixels = source_ref[f, pl.ds(row, STRIP), :].astype(F32)
            for t in range(blocks):
                at = (f * blocks + t) * STRIP
                z_ref[z, at : at + STRIP, :] = pixels[:, t * LANES : (t + 1) * LANES]
        for g in range(2):
            a = [z_ref[z, pl.ds(4 * g + p, rows, stride=STRIP), :] for p in range(4)]
            b = [None] * 4
            for p in (0, 2):
                b[p] = jnp.where(odd_chunk, pltpu.roll(a[p + 1], 32, 1), a[p])
                b[p + 1] = jnp.where(odd_chunk, a[p + 1], pltpu.roll(a[p], LANES - 32, 1))
            for p in (0, 1):
                low = jnp.where(high_chunk, pltpu.roll(b[p + 2], 64, 1), b[p])
                high = jnp.where(high_chunk, b[p + 2], pltpu.roll(b[p], LANES - 64, 1))
                for q, value in ((p, low), (p + 2, high)):
                    x_ref[slot, q * rows : (q + 1) * rows, g * LANES : (g + 1) * LANES] = value.astype(BF16)

    def store(lo_ref, hi_ref, slot, jj, lo, hi):
        lo_ref[slot, jj * rows : (jj + 1) * rows, :] = lo.astype(BF16)
        hi_ref[slot, (jj + 1) * rows : (jj + 2) * rows, :] = hi.astype(BF16)
        if jj == 0:
            up = jnp.where(group == blocks - 1, 0.0, pltpu.roll(lo, rows - 1, 0))
            lo_ref[slot, 16 * rows : 17 * rows, :] = up.astype(BF16)
        if jj == 15:
            down = jnp.where(group == 0, 0.0, pltpu.roll(hi, 1, 0))
            hi_ref[slot, 0:rows, :] = down.astype(BF16)

    def with_accumulators(*acc):
        count = m // CHUNK
        half = count // 2
        quads = [
            [[acc[2 * count * u + half * at + c] for c in range(half)] for u in range(2)]
            for at in range(4)
        ]

        def joined(*at):
            return [[ref for index in at for ref in quads[index][u]] for u in range(2)]

        decode_acc = joined(0)
        first_acc = (joined(0, 1), joined(0, 3))
        embed_acc = (joined(2, 3), joined(2, 1))
        second_acc = (joined(1, 2), joined(3, 2))

        def products(tiles):
            register = [0]

            def push(tile):
                for u in range(2):
                    pltpu.matmul_push_rhs(tile[0][u](), register[0] % 2, u)
                register[0] += 1

            units = []
            for at, tile in enumerate(tiles):
                for c in range(len(tile[1][0])):

                    def unit(at=at, tile=tile, c=c):
                        if c == 0:
                            if at == 0:
                                push(tile)
                            if at + 1 < len(tiles):
                                push(tiles[at + 1])
                        for u in range(2):
                            ref, operand = tile[1][u][c]
                            pltpu.matmul_acc_lhs(
                                ref, operand(), load_staged_rhs=at % 2 if c == 0 else None
                            )

                    units.append(unit)
            return units

        def conv_tiles(lo_ref, hi_ref, w_ref, accs, slots):
            tiles = []
            for k in range(4):
                side = k % 2
                weight = lambda k=k: w_ref[k * 256 : (k + 1) * 256, :]
                lists = []
                for u in range(2):
                    slot = slots[u + k // 2]
                    pairs = []
                    for c in range(count):

                        def operand(slot=slot, at=c * CHUNK, side=side):
                            if side == 0:
                                parts = (
                                    lo_ref[slot, at : at + CHUNK, :],
                                    hi_ref[slot, at + rows : at + rows + CHUNK, :],
                                )
                            else:
                                parts = (
                                    hi_ref[slot, at : at + CHUNK, :],
                                    lo_ref[slot, at + rows : at + rows + CHUNK, :],
                                )
                            return jnp.concatenate(parts, axis=1)

                        pairs.append((accs[u][c], operand))
                    lists.append(pairs)
                tiles.append(((weight, weight), lists))
            return tiles

        def conv_jobs(lo_ref, hi_ref, layer, accs, slots, finish):
            jobs = []
            for c in range(count):
                for u in range(2):

                    def job(c=c, u=u):
                        value = jnp.maximum(pltpu.matmul_pop(accs[u][c]) + bias_ref[layer + 1 : layer + 2, :], 0.0)
                        for r in range(per):
                            jj = c * per + r
                            halves = []
                            for h, (ref, shift) in enumerate(((lo_ref, 0), (hi_ref, rows))):
                                at = jj * rows + shift
                                below = ref[slots[u], at : at + rows, :].astype(F32)
                                above = ref[slots[u + 1], at : at + rows, :].astype(F32)
                                kept = (
                                    jnp.where(even, above, below)
                                    if layer == 0
                                    else jnp.where(even, below, above)
                                )
                                part = value[r * rows : (r + 1) * rows, h * LANES : (h + 1) * LANES]
                                halves.append(kept + part)
                            finish(u, jj, halves)

                    jobs.append(job)
            return jobs

        def embed_tiles(first, accs):
            tiles = []
            for k in range(2):
                weights, lists = [], []
                for u in range(2):
                    j = 2 * u + k
                    weights.append(lambda j=j: win_ref[:, j * 256 : (j + 1) * 256])
                    pairs = []
                    for c in range(patch_rows // CHUNK):

                        def operand(c=c):
                            s, at = c * CHUNK // (4 * rows), c * CHUNK % (4 * rows)
                            return x_ref[first + s, at : at + CHUNK, :]

                        pairs.append((accs[u][k * (patch_rows // CHUNK) + c], operand))
                    lists.append(pairs)
                tiles.append((weights, lists))
            return tiles

        def embed_jobs(slots, accs):
            jobs = []
            for k in range(2):
                for c in range(patch_rows // CHUNK):
                    for u in range(2):

                        def job(k=k, c=c, u=u):
                            j = 2 * u + k
                            ref = accs[u][k * (patch_rows // CHUNK) + c]
                            value = jnp.maximum(pltpu.matmul_pop(ref) + bias_ref[0:1, :], 0.0)
                            for r in range(per):
                                s, q = divmod(c * per + r, 4)
                                part = value[r * rows : (r + 1) * rows]
                                store(
                                    f0lo_ref, f0hi_ref, slots[s], 4 * q + j, part[:, 0:LANES], part[:, LANES:]
                                )

                        jobs.append(job)
            return jobs

        def decode_tiles():
            tiles = []
            for k in range(2):
                weights, lists = [], []
                for u in range(2):
                    tile = 2 * u + k
                    weights.append(lambda tile=tile: wd_ref[tile * 256 : (tile + 1) * 256, :])
                    lists.append(
                        [
                            (
                                decode_acc[u][c],
                                lambda c=c, tile=tile: f2_ref[
                                    c * CHUNK : (c + 1) * CHUNK, tile * 256 : (tile + 1) * 256
                                ],
                            )
                            for c in range(patch_rows // CHUNK)
                        ]
                    )
                tiles.append((weights, lists))
            return tiles

        def decode_jobs(first):
            jobs = []
            for c in range(patch_rows // CHUNK):

                def job(c=c):
                    s, at = c * CHUNK // (4 * rows), c * CHUNK % (4 * rows)
                    value = pltpu.matmul_pop(decode_acc[0][c]) + pltpu.matmul_pop(decode_acc[1][c])
                    pixels = x_ref[first + s + PAD - 1, at : at + CHUNK, :].astype(F32)
                    out_ref[first + s + 2, at : at + CHUNK, :] = (value + pixels).astype(BF16)

                jobs.append(job)
            return jobs

        def finish_second(u, jj, halves):
            q, j = jj // 4, jj % 4
            for h in range(2):
                at = j * 256 + h * LANES
                f2_ref[(4 * u + q) * rows : (4 * u + q + 1) * rows, at : at + LANES] = halves[h].astype(BF16)

        def step(n, parity, more):
            now = (0, 1) if parity == 0 else (2, 3)
            nxt = (2, 3) if parity == 0 else (0, 1)
            slots = (nxt[1],) + now
            before = (now[1],) + nxt
            scale = None
            if parity == 0:
                even_scale = jnp.where(n == steps - 1, bottom, 1.0)
                odd_scale = jnp.where(n == 0, top, 1.0)
                scale = jnp.where(even, even_scale, odd_scale)

            def finish_first(u, jj, halves):
                if u == 1 and scale is not None:
                    halves = [half * scale for half in halves]
                store(f1lo_ref, f1hi_ref, now[u], jj, *halves)

            jobs = conv_jobs(f1lo_ref, f1hi_ref, 1, second_acc[1 - parity], before, finish_second)
            if more:
                for s in range(2):

                    def job(s=s):
                        strip = jnp.minimum(2 * n + 4, total - 2)
                        row = pl.multiple_of(strip * STRIP, 2 * STRIP)
                        relayout(movie_ref, row + s * STRIP, strip + 1 + s + PAD, s)

                    jobs.append(job)
            accs = first_acc[parity]
            spread_jobs(products(conv_tiles(f0lo_ref, f0hi_ref, w1_ref, accs, slots)), jobs)
            tiles = (embed_tiles(2 * n + 2 + PAD, embed_acc[parity]) if more else []) + decode_tiles()
            jobs = conv_jobs(f0lo_ref, f0hi_ref, 0, accs, slots, finish_first)
            spread_jobs(products(tiles), jobs, 0 if more else count)
            jobs = (embed_jobs(nxt, embed_acc[parity]) if more else []) + decode_jobs(2 * n - 2)
            accs = second_acc[parity]
            spread_jobs(products(conv_tiles(f1lo_ref, f1hi_ref, w2_ref, accs, slots)), jobs, 0, 2)

        for ref in acc:
            pltpu.matmul_pop(ref)
        prepare(patch_in_ref, conv_ref, patch_out_ref, win_ref, w1_ref, w2_ref, wd_ref)
        bias_ref[0:1, :] = jnp.concatenate([patch_bias_ref[...]] * 4, axis=1)
        for layer in range(2):
            bias_ref[layer + 1 : layer + 2, :] = jnp.concatenate(
                [conv_bias_ref[layer : layer + 1, :]] * 4, axis=1
            )
        relayout(above_ref, 0, PAD, 0)
        relayout(below_ref, 0, total + 1 + PAD, 1)
        for strip in range(4):
            relayout(movie_ref, strip * STRIP, strip + 1 + PAD, strip % 2)
        spread_jobs(products(embed_tiles(PAD, embed_acc[0])), [])
        for job in embed_jobs((0, 1), embed_acc[0]):
            job()
        for ref in (f0lo_ref, f0hi_ref):
            ref[0] = (ref[0].astype(F32) * top).astype(BF16)

        def pair(i, carry):
            step(2 * i, 0, True)
            step(2 * i + 1, 1, True)
            return carry

        lax.fori_loop(0, (steps - 1) // 2, pair, 0)
        for ref in (f0lo_ref, f0hi_ref):
            ref[1] = (ref[1].astype(F32) * bottom).astype(BF16)
        step(steps - 1, 0, False)
        for job in conv_jobs(f1lo_ref, f1hi_ref, 1, second_acc[0], (3, 0, 1), finish_second):
            job()
        spread_jobs(products(decode_tiles()), [])
        for job in decode_jobs(2 * steps - 2):
            job()

    pl.run_scoped(
        with_accumulators,
        *[pltpu.ACC(u)((CHUNK, 256), F32) for u in range(2) for _ in range(2 * m // CHUNK)],
    )


def denoise(movie, above, below, patch_in, patch_bias, conv_weight, conv_bias, patch_out):
    frames, height, width = movie.shape
    total = height // STRIP
    rows = frames * (width // LANES)
    flops = 2 * total * rows * 16 * (2 * 1024 * 256 + 256 * 256 + 256 * 256)
    return pl.pallas_call(
        denoise_kernel,
        out_shape=jax.ShapeDtypeStruct((total + 4, 4 * rows, 256), BF16),
        scratch_shapes=[
            pltpu.VMEM((256, 1024), BF16),
            pltpu.VMEM((1024, 256), BF16),
            pltpu.VMEM((1024, 256), BF16),
            pltpu.VMEM((1024, 256), BF16),
            pltpu.VMEM((8, 256), F32),
            pltpu.VMEM((2, rows * STRIP, LANES), F32),
            pltpu.VMEM((total + 2 + PAD, 4 * rows, 256), BF16),
        ]
        + [pltpu.VMEM((4, 17 * rows, LANES), BF16)] * 4
        + [pltpu.VMEM((2 * 4 * rows, 1024), BF16)],
        compiler_params=pltpu.CompilerParams(vmem_limit_bytes=VMEM_BYTES),
        cost_estimate=pl.CostEstimate(flops=flops, bytes_accessed=8 << 20, transcendentals=0),
        name="denoise",
    )(movie, above, below, patch_in, patch_bias, conv_weight, conv_bias, patch_out)


def cells_kernel(frames, own, denoised_ref, footprint_ref, cell_ref, window_ref, out_ref):
    rows = denoised_ref.shape[1] // 4
    blocks = rows // frames
    slots = footprint_ref.shape[1]
    n = blocks * slots
    owned = out_ref.shape[0]
    kb = pl.program_id(0)

    def flat(ref):
        return jnp.concatenate([ref[pl.ds(kb * blocks + t, 1), :] for t in range(blocks)], axis=1)

    lhs = []
    for iw in range(4):
        lhs.append(
            jnp.concatenate([denoised_ref[16 * kb + 4 * iw + i4 + 4] for i4 in range(4)], axis=1)
        )
    weights = footprint_ref[...].reshape(n, footprint_ref.shape[2])
    every = lax.dot_general(jnp.concatenate(lhs, axis=0), weights, NT, preferred_element_type=F32)
    group = lax.broadcasted_iota(jnp.int32, (blocks, n), 0)
    block_of = lax.broadcasted_iota(jnp.int32, (1, n), 1) // slots
    target = flat(window_ref) * blocks + block_of
    sums = []
    for f in range(frames):
        total = jnp.zeros((blocks, n), F32)
        for w in range(16):
            at = w * rows + f * blocks
            total = total + jnp.where(target == group + w * blocks, every[at : at + blocks, :], 0.0)
        sums.append(jnp.sum(total, axis=0, keepdims=True))
    slot_sums = jnp.concatenate(sums, axis=0)
    cell = flat(cell_ref)
    owner = jnp.floor((cell.astype(F32) + 0.5) * (1.0 / own)).astype(jnp.int32)
    low = cell - owner * own
    row_owner = lax.broadcasted_iota(jnp.int32, (owned, n), 0) // frames
    onehot = jnp.where(lax.broadcasted_iota(jnp.int32, (own, n), 0) == low, 1.0, 0.0).astype(BF16)
    spread = jnp.where(
        row_owner == owner, jnp.concatenate([slot_sums] * (owned // frames), axis=0), 0.0
    )
    acc = None
    for _ in range(3):
        piece = spread.astype(BF16)
        spread = spread - piece.astype(F32)
        part = lax.dot_general(piece, onehot, NT, preferred_element_type=F32)
        acc = part if acc is None else acc + part

    @pl.when(kb == 0)
    def _():
        out_ref[...] = acc

    @pl.when(kb > 0)
    def _():
        out_ref[...] = out_ref[...] + acc


def cells(denoised, footprint, slot_cell, window, frames, own, owners):
    padded, rows4, _ = denoised.shape
    blocks = rows4 // (4 * frames)
    count, slots, pixels = footprint.shape
    whole = lambda a: pl.BlockSpec(a.shape, lambda n: (0,) * a.ndim)
    return pl.pallas_call(
        functools.partial(cells_kernel, frames, own),
        grid=(count // blocks,),
        in_specs=[
            whole(denoised),
            pl.BlockSpec((blocks, slots, pixels), lambda n: (n, 0, 0)),
            whole(slot_cell),
            whole(window),
        ],
        out_specs=pl.BlockSpec((owners * frames, own), lambda n: (0, 0)),
        out_shape=jax.ShapeDtypeStruct((owners * frames, own), F32),
        compiler_params=pltpu.CompilerParams(vmem_limit_bytes=VMEM_BYTES),
        cost_estimate=pl.CostEstimate(flops=2 << 30, bytes_accessed=5 << 20, transcendentals=0),
        name="cells",
    )(denoised, footprint, slot_cell, window)


def spikes_kernel(tm, tile, frames, moved_ref, decay_ref, out_ref):
    own = out_ref.shape[1]
    pieces = []
    for a in range(tm):
        total = jnp.zeros((frames, own), F32)
        for b in range(tile):
            at = (a * tile + b) * frames
            total = total + moved_ref[at : at + frames, :]
        pieces.append(total)
    traces = jnp.concatenate(pieces, axis=0)
    count = tm * frames
    centered = traces - jnp.sum(traces, axis=0, keepdims=True) * (1.0 / count)
    previous = jnp.concatenate([jnp.zeros((1, own), F32), centered[:-1]], axis=0)
    spikes = centered - decay_ref[...] * previous
    power = jnp.sum(spikes * spikes, axis=0, keepdims=True) * (1.0 / count)
    out_ref[...] = spikes / jnp.sqrt(power + 1e-05)


def body(
    movie,
    patch_in,
    patch_bias,
    conv_weight,
    conv_bias,
    patch_out,
    footprint,
    slot_cell,
    slot_window_index,
    decay,
):
    frames = movie.shape[0]
    own = decay.shape[0]
    tm, tile = lax.axis_size("tm"), lax.axis_size("tile")
    forward = [(i, i + 1) for i in range(tile - 1)]
    backward = [(target, source) for source, target in forward]
    above = lax.ppermute(movie[:, -STRIP:], "tile", forward)
    below = lax.ppermute(movie[:, :STRIP], "tile", backward)
    slots = lax.all_gather(footprint, "tm", axis=1, tiled=True)
    denoised = denoise(
        movie,
        above,
        below,
        patch_in,
        patch_bias[None, :],
        conv_weight,
        conv_bias,
        patch_out,
    )
    per_cell = cells(denoised, slots, slot_cell, slot_window_index, frames, own, tm * tile)
    moved = lax.all_to_all(per_cell, ("tm", "tile"), split_axis=0, concat_axis=0, tiled=True)
    return pl.pallas_call(
        functools.partial(spikes_kernel, tm, tile, frames),
        out_shape=jax.ShapeDtypeStruct((tm * frames, own), F32),
        name="spikes",
    )(moved, decay[None, :])


def solution(mesh):
    placed = (
        P(("field", "tm"), "tile", None),
        P(),
        P(),
        P(),
        P(),
        P(),
        P(("field", "tile"), "tm", None),
        P(("field", "tile"), None),
        P(("field", "tile"), None),
        P(("field", "tm", "tile")),
    )
    return jax.shard_map(
        body,
        mesh=mesh,
        in_specs=placed,
        out_specs=P(None, ("field", "tm", "tile")),
        check_vma=False,
    )
```

```python
import functools

import jax
import jax.numpy as jnp
from jax import lax
from jax.experimental import pallas as pl
from jax.experimental.pallas import tpu as pltpu
from jax.sharding import PartitionSpec as P

BLK = 128
LANES = 128
STRIP = 8
PAD = 3
CHUNK = 64
VMEM_BYTES = 60 << 20
NT = (((1,), (1,)), ((), ()))
F32 = jnp.float32
BF16 = jnp.bfloat16


def conv_taps(layer):
    blocks = []
    for d in range(2):
        for side in range(2):
            for x in range(2):
                for h_in in range(2):
                    in_row = 2 * (d - 1) + h_in if layer % 2 == 0 else 2 * d - h_in
                    in_col = x if side == 0 else (-1, 2)[x]
                    row = []
                    for c in range(2):
                        for h_out in range(2):
                            out_row = -h_out if layer % 2 == 0 else h_out
                            tap_r, tap_c = in_row - out_row + 1, in_col - c + 1
                            ok = 0 <= tap_r <= 2 and 0 <= tap_c <= 2
                            row.append(3 * tap_r + tap_c if ok else None)
                    blocks.append(row)
    return blocks


def prepare(patch_in_ref, conv_ref, patch_out_ref, win_ref, w1_ref, w2_ref, wd_ref):
    chan = patch_in_ref.shape[1]

    def spread(taps):
        parts = [jnp.concatenate([taps[4 * a : 4 * a + 4]] * 8, axis=0) for a in range(4)]
        return jnp.concatenate(parts * 2, axis=0)

    spread_in = spread(patch_in_ref[...].astype(F32))
    spread_out = spread(patch_out_ref[...].astype(F32).T).T
    k = lax.broadcasted_iota(jnp.int32, (256, 2 * chan), 0)
    lane = lax.broadcasted_iota(jnp.int32, (256, 2 * chan), 1)
    wide_in = jnp.concatenate([spread_in, spread_in], axis=1)
    for pair in range(8):
        keep = ((k % 32) // 4 == pair) & (k // 128 == lane // chan)
        win_ref[:, pair * 2 * chan : (pair + 1) * 2 * chan] = jnp.where(keep, wide_in, 0.0).astype(BF16)
    k = lax.broadcasted_iota(jnp.int32, (2 * chan, 256), 1)
    half = lax.broadcasted_iota(jnp.int32, (2 * chan, 256), 0) // chan
    wide_out = jnp.concatenate([spread_out, spread_out], axis=0)
    for pair in range(8):
        keep = ((k % 32) // 4 == pair) & (k // 128 == half)
        wd_ref[pair * 2 * chan : (pair + 1) * 2 * chan, :] = jnp.where(keep, wide_out, 0.0).astype(BF16)
    blank = jnp.zeros((chan, chan), F32)
    for layer, out in enumerate((w1_ref, w2_ref)):
        turned = [conv_ref[layer, tap].astype(F32).T for tap in range(9)]
        for row, taps in enumerate(conv_taps(layer)):
            for c in range(2):
                pair = [blank if taps[2 * c + h] is None else turned[taps[2 * c + h]] for h in range(2)]
                out[row * chan : (row + 1) * chan, c * LANES : (c + 1) * LANES] = jnp.concatenate(
                    pair, axis=1
                ).astype(BF16)


def spread_jobs(units, jobs, lead=0, rate=None):
    done = 0
    for at, unit in enumerate(units):
        want = lead + (at * (len(jobs) - lead) // len(units) if rate is None else at * rate)
        while done < min(want, len(jobs)):
            jobs[done]()
            done += 1
        unit()
    for job in jobs[done:]:
        job()


def denoise_kernel(
    movie_ref,
    above_ref,
    below_ref,
    patch_in_ref,
    patch_bias_ref,
    conv_ref,
    conv_bias_ref,
    patch_out_ref,
    out_ref,
    win_ref,
    w1_ref,
    w2_ref,
    wd_ref,
    bias_ref,
    z_ref,
    x_ref,
    f0lo_ref,
    f0hi_ref,
    f1lo_ref,
    f1hi_ref,
    f2_ref,
):
    frames = movie_ref.shape[0]
    total = movie_ref.shape[1] // STRIP
    blocks = movie_ref.shape[2] // LANES
    rows = frames * blocks
    m = 16 * rows
    patch_rows = 2 * 4 * rows
    steps = total // 2 + 1
    lane = lax.broadcasted_iota(jnp.int32, (rows, LANES), 1)
    group = lax.broadcasted_iota(jnp.int32, (rows, LANES), 0) % blocks
    odd_chunk = (lane // 32) % 2 == 1
    high_chunk = lane // 64 == 1
    even = lane < 64
    place = lax.axis_index("tile")
    top = jnp.where(place > 0, 1.0, 0.0)
    bottom = jnp.where(place < lax.axis_size("tile") - 1, 1.0, 0.0)
    per = CHUNK // rows

    def relayout(source_ref, row, slot, z):
        for f in range(frames):
            pixels = source_ref[f, pl.ds(row, STRIP), :].astype(F32)
            for t in range(blocks):
                at = (f * blocks + t) * STRIP
                z_ref[z, at : at + STRIP, :] = pixels[:, t * LANES : (t + 1) * LANES]
        for g in range(2):
            a = [z_ref[z, pl.ds(4 * g + p, rows, stride=STRIP), :] for p in range(4)]
            b = [None] * 4
            for p in (0, 2):
                b[p] = jnp.where(odd_chunk, pltpu.roll(a[p + 1], 32, 1), a[p])
                b[p + 1] = jnp.where(odd_chunk, a[p + 1], pltpu.roll(a[p], LANES - 32, 1))
            for p in (0, 1):
                low = jnp.where(high_chunk, pltpu.roll(b[p + 2], 64, 1), b[p])
                high = jnp.where(high_chunk, b[p + 2], pltpu.roll(b[p], LANES - 64, 1))
                for q, value in ((p, low), (p + 2, high)):
                    x_ref[slot, q * rows : (q + 1) * rows, g * LANES : (g + 1) * LANES] = value.astype(BF16)

    def store(lo_ref, hi_ref, slot, jj, lo, hi):
        lo_ref[slot, jj * rows : (jj + 1) * rows, :] = lo.astype(BF16)
        hi_ref[slot, (jj + 1) * rows : (jj + 2) * rows, :] = hi.astype(BF16)
        if jj == 0:
            up = jnp.where(group == blocks - 1, 0.0, pltpu.roll(lo, rows - 1, 0))
            lo_ref[slot, 16 * rows : 17 * rows, :] = up.astype(BF16)
        if jj == 15:
            down = jnp.where(group == 0, 0.0, pltpu.roll(hi, 1, 0))
            hi_ref[slot, 0:rows, :] = down.astype(BF16)

    def with_accumulators(*acc):
        count = m // CHUNK
        half = count // 2
        quads = [
            [[acc[2 * count * u + half * at + c] for c in range(half)] for u in range(2)]
            for at in range(4)
        ]

        def joined(*at):
            return [[ref for index in at for ref in quads[index][u]] for u in range(2)]

        decode_acc = joined(0)
        first_acc = (joined(0, 1), joined(0, 3))
        embed_acc = (joined(2, 3), joined(2, 1))
        second_acc = (joined(1, 2), joined(3, 2))

        def products(tiles):
            register = [0]

            def push(tile):
                for u in range(2):
                    pltpu.matmul_push_rhs(tile[0][u](), register[0] % 2, u)
                register[0] += 1

            units = []
            for at, tile in enumerate(tiles):
                for c in range(len(tile[1][0])):

                    def unit(at=at, tile=tile, c=c):
                        if c == 0:
                            if at == 0:
                                push(tile)
                            if at + 1 < len(tiles):
                                push(tiles[at + 1])
                        for u in range(2):
                            ref, operand = tile[1][u][c]
                            pltpu.matmul_acc_lhs(
                                ref, operand(), load_staged_rhs=at % 2 if c == 0 else None
                            )

                    units.append(unit)
            return units

        def conv_tiles(lo_ref, hi_ref, w_ref, accs, slots):
            tiles = []
            for k in range(4):
                side = k % 2
                weight = lambda k=k: w_ref[k * 256 : (k + 1) * 256, :]
                lists = []
                for u in range(2):
                    slot = slots[u + k // 2]
                    pairs = []
                    for c in range(count):

                        def operand(slot=slot, at=c * CHUNK, side=side):
                            if side == 0:
                                parts = (
                                    lo_ref[slot, at : at + CHUNK, :],
                                    hi_ref[slot, at + rows : at + rows + CHUNK, :],
                                )
                            else:
                                parts = (
                                    hi_ref[slot, at : at + CHUNK, :],
                                    lo_ref[slot, at + rows : at + rows + CHUNK, :],
                                )
                            return jnp.concatenate(parts, axis=1)

                        pairs.append((accs[u][c], operand))
                    lists.append(pairs)
                tiles.append(((weight, weight), lists))
            return tiles

        def conv_jobs(lo_ref, hi_ref, layer, accs, slots, finish):
            jobs = []
            for c in range(count):
                for u in range(2):

                    def job(c=c, u=u):
                        value = jnp.maximum(pltpu.matmul_pop(accs[u][c]) + bias_ref[layer + 1 : layer + 2, :], 0.0)
                        for r in range(per):
                            jj = c * per + r
                            halves = []
                            for h, (ref, shift) in enumerate(((lo_ref, 0), (hi_ref, rows))):
                                at = jj * rows + shift
                                below = ref[slots[u], at : at + rows, :].astype(F32)
                                above = ref[slots[u + 1], at : at + rows, :].astype(F32)
                                kept = (
                                    jnp.where(even, above, below)
                                    if layer == 0
                                    else jnp.where(even, below, above)
                                )
                                part = value[r * rows : (r + 1) * rows, h * LANES : (h + 1) * LANES]
                                halves.append(kept + part)
                            finish(u, jj, halves)

                    jobs.append(job)
            return jobs

        def embed_tiles(first, accs):
            tiles = []
            for k in range(2):
                weights, lists = [], []
                for u in range(2):
                    j = 2 * u + k
                    weights.append(lambda j=j: win_ref[:, j * 256 : (j + 1) * 256])
                    pairs = []
                    for c in range(patch_rows // CHUNK):

                        def operand(c=c):
                            s, at = c * CHUNK // (4 * rows), c * CHUNK % (4 * rows)
                            return x_ref[first + s, at : at + CHUNK, :]

                        pairs.append((accs[u][k * (patch_rows // CHUNK) + c], operand))
                    lists.append(pairs)
                tiles.append((weights, lists))
            return tiles

        def embed_jobs(slots, accs):
            jobs = []
            for k in range(2):
                for c in range(patch_rows // CHUNK):
                    for u in range(2):

                        def job(k=k, c=c, u=u):
                            j = 2 * u + k
                            ref = accs[u][k * (patch_rows // CHUNK) + c]
                            value = jnp.maximum(pltpu.matmul_pop(ref) + bias_ref[0:1, :], 0.0)
                            for r in range(per):
                                s, q = divmod(c * per + r, 4)
                                part = value[r * rows : (r + 1) * rows]
                                store(
                                    f0lo_ref, f0hi_ref, slots[s], 4 * q + j, part[:, 0:LANES], part[:, LANES:]
                                )

                        jobs.append(job)
            return jobs

        def decode_tiles():
            tiles = []
            for k in range(2):
                weights, lists = [], []
                for u in range(2):
                    tile = 2 * u + k
                    weights.append(lambda tile=tile: wd_ref[tile * 256 : (tile + 1) * 256, :])
                    lists.append(
                        [
                            (
                                decode_acc[u][c],
                                lambda c=c, tile=tile: f2_ref[
                                    c * CHUNK : (c + 1) * CHUNK, tile * 256 : (tile + 1) * 256
                                ],
                            )
                            for c in range(patch_rows // CHUNK)
                        ]
                    )
                tiles.append((weights, lists))
            return tiles

        def decode_jobs(first):
            jobs = []
            for c in range(patch_rows // CHUNK):

                def job(c=c):
                    s, at = c * CHUNK // (4 * rows), c * CHUNK % (4 * rows)
                    value = pltpu.matmul_pop(decode_acc[0][c]) + pltpu.matmul_pop(decode_acc[1][c])
                    pixels = x_ref[first + s + PAD - 1, at : at + CHUNK, :].astype(F32)
                    out_ref[first + s + 2, at : at + CHUNK, :] = (value + pixels).astype(BF16)

                jobs.append(job)
            return jobs

        def finish_second(u, jj, halves):
            q, j = jj // 4, jj % 4
            for h in range(2):
                at = j * 256 + h * LANES
                f2_ref[(4 * u + q) * rows : (4 * u + q + 1) * rows, at : at + LANES] = halves[h].astype(BF16)

        def step(n, parity, more):
            now = (0, 1) if parity == 0 else (2, 3)
            nxt = (2, 3) if parity == 0 else (0, 1)
            slots = (nxt[1],) + now
            before = (now[1],) + nxt
            scale = None
            if parity == 0:
                even_scale = jnp.where(n == steps - 1, bottom, 1.0)
                odd_scale = jnp.where(n == 0, top, 1.0)
                scale = jnp.where(even, even_scale, odd_scale)

            def finish_first(u, jj, halves):
                if u == 1 and scale is not None:
                    halves = [half * scale for half in halves]
                store(f1lo_ref, f1hi_ref, now[u], jj, *halves)

            jobs = conv_jobs(f1lo_ref, f1hi_ref, 1, second_acc[1 - parity], before, finish_second)
            if more:
                for s in range(2):

                    def job(s=s):
                        strip = jnp.minimum(2 * n + 4, total - 2)
                        row = pl.multiple_of(strip * STRIP, 2 * STRIP)
                        relayout(movie_ref, row + s * STRIP, strip + 1 + s + PAD, s)

                    jobs.append(job)
            accs = first_acc[parity]
            spread_jobs(products(conv_tiles(f0lo_ref, f0hi_ref, w1_ref, accs, slots)), jobs)
            tiles = (embed_tiles(2 * n + 2 + PAD, embed_acc[parity]) if more else []) + decode_tiles()
            jobs = conv_jobs(f0lo_ref, f0hi_ref, 0, accs, slots, finish_first)
            spread_jobs(products(tiles), jobs, 0 if more else count)
            jobs = (embed_jobs(nxt, embed_acc[parity]) if more else []) + decode_jobs(2 * n - 2)
            accs = second_acc[parity]
            spread_jobs(products(conv_tiles(f1lo_ref, f1hi_ref, w2_ref, accs, slots)), jobs, 0, 2)

        for ref in acc:
            pltpu.matmul_pop(ref)
        prepare(patch_in_ref, conv_ref, patch_out_ref, win_ref, w1_ref, w2_ref, wd_ref)
        bias_ref[0:1, :] = jnp.concatenate([patch_bias_ref[...]] * 4, axis=1)
        for layer in range(2):
            bias_ref[layer + 1 : layer + 2, :] = jnp.concatenate(
                [conv_bias_ref[layer : layer + 1, :]] * 4, axis=1
            )
        relayout(above_ref, 0, PAD, 0)
        relayout(below_ref, 0, total + 1 + PAD, 1)
        for strip in range(4):
            relayout(movie_ref, strip * STRIP, strip + 1 + PAD, strip % 2)
        spread_jobs(products(embed_tiles(PAD, embed_acc[0])), [])
        for job in embed_jobs((0, 1), embed_acc[0]):
            job()
        for ref in (f0lo_ref, f0hi_ref):
            ref[0] = (ref[0].astype(F32) * top).astype(BF16)

        def pair(i, carry):
            step(2 * i, 0, True)
            step(2 * i + 1, 1, True)
            return carry

        lax.fori_loop(0, (steps - 1) // 2, pair, 0)
        for ref in (f0lo_ref, f0hi_ref):
            ref[1] = (ref[1].astype(F32) * bottom).astype(BF16)
        step(steps - 1, 0, False)
        for job in conv_jobs(f1lo_ref, f1hi_ref, 1, second_acc[0], (3, 0, 1), finish_second):
            job()
        spread_jobs(products(decode_tiles()), [])
        for job in decode_jobs(2 * steps - 2):
            job()

    pl.run_scoped(
        with_accumulators,
        *[pltpu.ACC(u)((CHUNK, 256), F32) for u in range(2) for _ in range(2 * m // CHUNK)],
    )


def denoise(movie, above, below, patch_in, patch_bias, conv_weight, conv_bias, patch_out):
    frames, height, width = movie.shape
    total = height // STRIP
    rows = frames * (width // LANES)
    flops = 2 * total * rows * 16 * (2 * 1024 * 256 + 256 * 256 + 256 * 256)
    return pl.pallas_call(
        denoise_kernel,
        out_shape=jax.ShapeDtypeStruct((total + 4, 4 * rows, 256), BF16),
        scratch_shapes=[
            pltpu.VMEM((256, 1024), BF16),
            pltpu.VMEM((1024, 256), BF16),
            pltpu.VMEM((1024, 256), BF16),
            pltpu.VMEM((1024, 256), BF16),
            pltpu.VMEM((8, 256), F32),
            pltpu.VMEM((2, rows * STRIP, LANES), F32),
            pltpu.VMEM((total + 2 + PAD, 4 * rows, 256), BF16),
        ]
        + [pltpu.VMEM((4, 17 * rows, LANES), BF16)] * 4
        + [pltpu.VMEM((2 * 4 * rows, 1024), BF16)],
        compiler_params=pltpu.CompilerParams(vmem_limit_bytes=VMEM_BYTES),
        cost_estimate=pl.CostEstimate(flops=flops, bytes_accessed=8 << 20, transcendentals=0),
        name="denoise",
    )(movie, above, below, patch_in, patch_bias, conv_weight, conv_bias, patch_out)


def cells_kernel(frames, own, denoised_ref, cell_ref, window_ref, *refs):
    pieces = refs[:-5]
    out_ref, image_ref, weights_ref, image_sem, piece_sem = refs[-5:]
    total = denoised_ref.shape[0] - 4
    rows = denoised_ref.shape[1] // 4
    blocks = rows // frames
    share = pieces[0].shape[1]
    slots = share * len(pieces)
    n = blocks * slots
    owners = out_ref.shape[0]
    place = lax.axis_index("tm")

    def copies(kb):
        strips, squares = pl.ds(16 * kb, 16), pl.ds(kb * blocks, blocks)
        yield pltpu.make_async_copy(
            denoised_ref.at[pl.ds(16 * kb + 4, 16)], image_ref.at[strips], image_sem.at[kb]
        )
        for at, piece in enumerate(pieces):
            first = pl.multiple_of(lax.rem(place + at, len(pieces)) * share, share)
            yield pltpu.make_async_copy(
                piece.at[squares], weights_ref.at[squares, pl.ds(first, share)], piece_sem.at[kb, at]
            )

    for kb in range(total // 16):
        for copy in copies(kb):
            copy.start()

    group = lax.broadcasted_iota(jnp.int32, (blocks, n), 0)
    block_of = lax.broadcasted_iota(jnp.int32, (1, n), 1) // slots
    row_owner = lax.broadcasted_iota(jnp.int32, (owners * frames, n), 0) // frames
    acc = None
    for kb in range(total // 16):

        def flat(ref):
            return jnp.concatenate([ref[kb * blocks + t : kb * blocks + t + 1, :] for t in range(blocks)], axis=1)

        target = flat(window_ref) * blocks + block_of
        cell = flat(cell_ref)
        owner = jnp.floor((cell.astype(F32) + 0.5) * (1.0 / own)).astype(jnp.int32)
        low = cell - owner * own
        onehot = jnp.where(lax.broadcasted_iota(jnp.int32, (own, n), 0) == low, 1.0, 0.0).astype(BF16)
        for copy in copies(kb):
            copy.wait()
        lhs = []
        for iw in range(4):
            lhs.append(
                jnp.concatenate([image_ref[16 * kb + 4 * iw + i4] for i4 in range(4)], axis=1)
            )
        weights = weights_ref[kb * blocks : (kb + 1) * blocks].reshape(n, weights_ref.shape[2])
        every = lax.dot_general(jnp.concatenate(lhs, axis=0), weights, NT, preferred_element_type=F32)
        sums = []
        for f in range(frames):
            picked = jnp.zeros((blocks, n), F32)
            for w in range(16):
                at = w * rows + f * blocks
                picked = picked + jnp.where(
                    target == group + w * blocks, every[at : at + blocks, :], 0.0
                )
            sums.append(jnp.sum(picked, axis=0, keepdims=True))
        slot_sums = jnp.concatenate(sums, axis=0)
        spread = jnp.where(row_owner == owner, jnp.concatenate([slot_sums] * owners, axis=0), 0.0)
        for _ in range(3):
            piece = spread.astype(BF16)
            spread = spread - piece.astype(F32)
            part = lax.dot_general(piece, onehot, NT, preferred_element_type=F32)
            acc = part if acc is None else acc + part
    for o in range(owners):
        out_ref[o] = acc[o * frames : (o + 1) * frames]


def cells(denoised, pieces, slot_cell, window, frames, own, owners):
    padded, rows4, _ = denoised.shape
    count, share, pixels = pieces[0].shape
    steps = (padded - 4) // 16
    away = pl.BlockSpec(memory_space=pl.ANY)
    here = pl.BlockSpec(memory_space=pltpu.VMEM)
    return pl.pallas_call(
        functools.partial(cells_kernel, frames, own),
        in_specs=[away, here, here] + [away] * len(pieces),
        out_shape=jax.ShapeDtypeStruct((owners, frames, own), F32),
        scratch_shapes=[
            pltpu.VMEM((padded - 4, rows4, 256), BF16),
            pltpu.VMEM((count, share * len(pieces), pixels), BF16),
            pltpu.SemaphoreType.DMA((steps,)),
            pltpu.SemaphoreType.DMA((steps, len(pieces))),
        ],
        compiler_params=pltpu.CompilerParams(vmem_limit_bytes=VMEM_BYTES),
        cost_estimate=pl.CostEstimate(flops=2 << 30, bytes_accessed=5 << 20, transcendentals=0),
        name="cells",
    )(denoised, slot_cell, window, *pieces)


def spikes_kernel(tm, tile, frames, moved_ref, decay_ref, out_ref):
    own = out_ref.shape[1]
    pieces = []
    for a in range(tm):
        total = jnp.zeros((frames, own), F32)
        for b in range(tile):
            total = total + moved_ref[a * tile + b]
        pieces.append(total)
    traces = jnp.concatenate(pieces, axis=0)
    count = tm * frames
    centered = traces - jnp.sum(traces, axis=0, keepdims=True) * (1.0 / count)
    previous = jnp.concatenate([jnp.zeros((1, own), F32), centered[:-1]], axis=0)
    spikes = centered - decay_ref[...] * previous
    power = jnp.sum(spikes * spikes, axis=0, keepdims=True) * (1.0 / count)
    out_ref[...] = spikes / jnp.sqrt(power + 1e-05)


def body(
    movie,
    patch_in,
    patch_bias,
    conv_weight,
    conv_bias,
    patch_out,
    footprint,
    slot_cell,
    slot_window_index,
    decay,
):
    frames = movie.shape[0]
    own = decay.shape[0]
    tm, tile = lax.axis_size("tm"), lax.axis_size("tile")
    forward = [(i, i + 1) for i in range(tile - 1)]
    backward = [(target, source) for source, target in forward]
    above = lax.ppermute(movie[:, -STRIP:], "tile", forward)
    below = lax.ppermute(movie[:, :STRIP], "tile", backward)
    pieces = [footprint]
    for ahead in range(1, tm):
        ring = [(source, (source - ahead) % tm) for source in range(tm)]
        pieces.append(lax.ppermute(footprint, "tm", ring))
    denoised = denoise(
        movie,
        above,
        below,
        patch_in,
        patch_bias[None, :],
        conv_weight,
        conv_bias,
        patch_out,
    )
    per_cell = cells(denoised, pieces, slot_cell, slot_window_index, frames, own, tm * tile)
    moved = lax.all_to_all(per_cell, ("tm", "tile"), split_axis=0, concat_axis=0, tiled=True)
    return pl.pallas_call(
        functools.partial(spikes_kernel, tm, tile, frames),
        out_shape=jax.ShapeDtypeStruct((tm * frames, own), F32),
        name="spikes",
    )(moved, decay[None, :])


def solution(mesh):
    placed = (
        P(("field", "tm"), "tile", None),
        P(),
        P(),
        P(),
        P(),
        P(),
        P(("field", "tile"), "tm", None),
        P(("field", "tile"), None),
        P(("field", "tile"), None),
        P(("field", "tm", "tile")),
    )
    return jax.shard_map(
        body,
        mesh=mesh,
        in_specs=placed,
        out_specs=P(None, ("field", "tm", "tile")),
        check_vma=False,
    )
```
